512 devices in a mesh: member: 4 (over y_hi), lat: 8 (over x, core), lon: 16 (over z, y_lo).
Axes of the slice: x: 4, y: 8 (y_hi: 4, y_lo: 2; y = y_hi * 2 + y_lo), z: 8, core: 2. Of those that a mesh axis runs over, the one named last changes fastest.
Arguments:
- inputs: bfloat16 [4, 96, 8, 16, 5760], P('member', None, 'lat', 'lon'), may hold values from -6 to 6
- weight: bfloat16 [9, 8064], replicated, may hold values from -0.21875 to 0.21875
- bias: float32 [84], replicated, may hold values from -3 to 3
- analysis: bfloat16 [84, 8, 16, 5760], P(None, 'lat', 'lon'), may hold values from -7 to 7
- field_weight: float32 [84], replicated, may hold values from 0.25 to 2.5
Outputs:
- grad_input: bfloat16 [4, 96, 8, 16, 5760], P('member', None, 'lat', 'lon')
- grad_weight: float32 [9, 8064], replicated
- grad_bias: float32 [84], replicated
The draws below stay inside these ranges and needn't reach their ends.
All inputs are finite; a program needn't handle non-finite values.
Results may differ from the reference program's by a relative error of at most 0.0053.
Values may be sent and summed in bfloat16 or wider, within the bound.
A program may use at most 128 MiB of HBM per device.

```python
import math
import jax
import jax.numpy as jnp
from jax import lax

C = 96
F = 84
NLON = 1440
LAT_DEV = 64
MEMBERS = 4
CELLS_DEV = 5760
N_LAT = 8
N_LON = 16


def level_of(own_key, shape, pieces, smallest, high):
    def one(position, blocks):
        draws = jax.random.uniform(jax.random.fold_in(jax.random.fold_in(own_key, 6), position), (blocks,), jnp.float32, smallest / len(pieces), high / len(pieces))
        return jnp.repeat(jnp.exp(draws), shape[position] // blocks).reshape((-1,) + (1,) * (len(shape) - position - 1))

    level = one(*pieces[0])
    for cut in pieces[1:]:
        level = level * one(*cut)
    return level


def bell_draw(rng, extent, spread, most, pieces=(), held_as=jnp.bfloat16):
    entries = spread * jax.random.normal(rng, extent, jnp.float32)
    if pieces:
        entries = entries * level_of(rng, extent, pieces, -0.22, 0.18)
    return jnp.clip(entries, -most, most).astype(held_as)


def setup_inputs(seed: int = 0) -> dict:
    key_list = jax.random.split(jax.random.key(seed), 6)
    inputs = bell_draw(key_list[0], (MEMBERS, C, N_LAT, N_LON, CELLS_DEV), 1.0, 6.0, ((0, 4), (2, 8), (3, 16)))
    weight = bell_draw(key_list[1], (9, C * F), (9 * C) ** -0.5, 0.21875)
    bias = bell_draw(key_list[2], (F,), 0.5, 3.0, (), jnp.float32)
    analysis = bell_draw(key_list[3], (F, N_LAT, N_LON, CELLS_DEV), 1.2, 7.0, ((1, 8), (2, 16)))
    field_weight = jnp.clip(jnp.exp(jax.random.uniform(key_list[4], (F,), jnp.float32, math.log(0.25), math.log(2.5))), 0.25, 2.5)
    return dict(inputs=inputs, weight=weight, bias=bias, analysis=analysis, field_weight=field_weight)


def to_grid(blocked):
    lead = blocked.shape[:-3]
    lon_cols = NLON // N_LON
    shaped = blocked.reshape(lead + (N_LAT, N_LON, LAT_DEV, lon_cols))
    rank = len(lead)
    order = tuple(range(rank)) + (rank, rank + 2, rank + 1, rank + 3)
    return jnp.transpose(shaped, order).reshape(lead + (N_LAT * LAT_DEV, NLON))

def to_blocks(grid_field):
    lead = grid_field.shape[:-2]
    lon_cols = NLON // N_LON
    shaped = grid_field.reshape(lead + (N_LAT, LAT_DEV, N_LON, lon_cols))
    rank = len(lead)
    order = tuple(range(rank)) + (rank, rank + 2, rank + 1, rank + 3)
    return jnp.transpose(shaped, order).reshape(lead + (N_LAT, N_LON, LAT_DEV * lon_cols))

def pad_grid(grid_field):
    wrapped = jnp.concatenate([grid_field[:, :, -1:], grid_field, grid_field[:, :, :1]], axis=2)
    return jnp.pad(wrapped, ((0, 0), (1, 1), (0, 0)))

def kernel_slope(values):
    return values * lax.rsqrt(values * values + 1.0)

def reference(inputs, weight, bias, analysis, field_weight):
    inputs = to_grid(inputs)
    analysis = to_grid(analysis)
    members = inputs.shape[0]
    lat_count = analysis.shape[1]
    lon_count = analysis.shape[2]
    cell_count = lat_count * lon_count
    tap_weights = weight.reshape(9, C, F)

    def forward(member_field):
        padded = pad_grid(member_field)
        summed_terms = jnp.zeros((F, cell_count), jnp.float32)
        for tap_index in range(9):
            row_off = tap_index // 3
            col_off = tap_index % 3
            window = padded[:, row_off:row_off + lat_count, col_off:col_off + lon_count].reshape(C, cell_count)
            summed_terms = summed_terms + jnp.dot(tap_weights[tap_index].T, window, preferred_element_type=jnp.float32)
        summed_terms = summed_terms + bias[:, None]
        return summed_terms.astype(jnp.bfloat16).reshape(F, lat_count, lon_count)
    prediction = lax.map(forward, inputs)
    target = analysis.astype(jnp.float32)
    gradients = []
    for member_index in range(members):
        own_values = prediction[member_index].astype(jnp.float32)
        pair_slope = jnp.zeros_like(own_values)
        for other_index in range(members):
            pair_slope = pair_slope + kernel_slope(own_values - prediction[other_index].astype(jnp.float32))
        target_slope = kernel_slope(own_values - target)
        member_grad = field_weight[:, None, None] * (target_slope / members - pair_slope / (members * (members - 1)))
        gradients.append(member_grad.astype(jnp.bfloat16))
    score_grad = jnp.stack(gradients)

    def backward(pair_args):
        member_field, pred_grad = pair_args
        padded = pad_grid(member_field)
        grad_padded = pad_grid(pred_grad)
        grad_flat = pred_grad.reshape(F, cell_count)
        input_terms = jnp.zeros((C, cell_count), jnp.float32)
        weight_terms = []
        for tap_index in range(9):
            row_off = tap_index // 3
            col_off = tap_index % 3
            window = padded[:, row_off:row_off + lat_count, col_off:col_off + lon_count].reshape(C, cell_count)
            weight_terms.append(lax.dot_general(window, grad_flat, (((1,), (1,)), ((), ())), preferred_element_type=jnp.float32))
            grad_window = grad_padded[:, 2 - row_off:2 - row_off + lat_count, 2 - col_off:2 - col_off + lon_count].reshape(F, cell_count)
            input_terms = input_terms + jnp.dot(tap_weights[tap_index], grad_window, preferred_element_type=jnp.float32)
        bias_terms = lax.optimization_barrier(jnp.sum(pred_grad.astype(jnp.float32), axis=(1, 2)))
        return (input_terms.astype(jnp.bfloat16).reshape(C, lat_count, lon_count), jnp.stack(weight_terms), bias_terms)
    grad_input, weight_parts, bias_parts = lax.map(backward, (inputs, score_grad))
    grad_weight = (lax.optimization_barrier(jnp.sum(weight_parts, axis=0)) / cell_count).reshape(9, C * F)
    grad_bias = lax.optimization_barrier(jnp.sum(bias_parts, axis=0)) / cell_count
    return (to_blocks(grad_input), grad_weight, grad_bias)
```

```python
import numpy as np
import jax
import jax.numpy as jnp
from jax import lax
from jax.experimental import pallas as pl
from jax.experimental.pallas import tpu as pltpu
from jax.sharding import PartitionSpec as P

MESH = pl.DeviceIdType.MESH
C, F, ROWS, COLS = 96, 84, 64, 90
CELLS = ROWS * COLS
PITCH = COLS + 2
PAIRS = 24
CHUNKS = 6
STACK = 896
BF, F32 = jnp.bfloat16, jnp.float32
TAPS = [(a, b) for a in range(3) for b in range(3)]


def padded_source():
    lane = np.arange(PAIRS * 256)
    r, c = lane // PITCH, lane % PITCH
    inside = (r >= 1) & (r <= ROWS) & (c >= 1) & (c <= COLS)
    return np.where(inside, COLS * (r - 1) + c - 1, -1)


def dense_source():
    cell = np.arange(CELLS)
    return PITCH * (cell // COLS + 1) + cell % COLS + 1


def segments(source, tile):
    out = []
    for lane in range(128):
        src = source[tile * 128 + lane]
        key = (None, 0) if src < 0 else (int(src) // 128, int(lane - src) % 128)
        if not out or out[-1][1:] != key:
            out.append((lane,) + key)
    return out


def move_tile(source, tile, load, rows):
    lane = lax.broadcasted_iota(jnp.int32, (rows, 128), 1)
    acc = None
    for first, src, shift in segments(source, tile):
        if src is None:
            val = jnp.zeros((rows, 128), BF)
        else:
            val = load(src)
            if shift:
                val = pltpu.roll(val, shift, 1)
        acc = val if acc is None else jnp.where(lane >= first, val, acc)
    return acc


def lane_grid(p):
    o = p * 256 + lax.broadcasted_iota(jnp.int32, (1, 256), 1)
    r = lax.shift_right_logical(o * 45591, 22)
    c = o - r * PITCH
    return r, c


def interior(p):
    r, c = lane_grid(p)
    return (r >= 1) & (r <= ROWS) & (c >= 1) & (c <= COLS)


def slope(u):
    return u * lax.rsqrt(u * u + 1.0)


def edge_columns(grid):
    lane = lax.broadcasted_iota(jnp.int32, (C, 128), 1)
    first = last = jnp.zeros((C, 128), BF)
    for r in range(1, ROWS + 1):
        for col in (1, COLS):
            o = PITCH * r + col
            t, l = o // 128, o % 128
            val = grid[t // 2 + 1, t % 2]
            val = pltpu.roll(val, (r - l) % 128, 1)
            if col == 1:
                first = jnp.where(lane == r, val, first)
            else:
                last = jnp.where(lane == r, val, last)
    return first, last


def place_halo(grid, row_top, row_bottom, left, right, lat, n_lat):
    lane = lax.broadcasted_iota(jnp.int32, (C, 128), 1)
    zero = jnp.zeros((C, 128), BF)
    has_top = jnp.where(lat > 0, 1, 0)
    has_bottom = jnp.where(lat < n_lat - 1, 1, 0)
    top_on = jnp.broadcast_to(has_top, (C, 128)) == 1
    bottom_on = jnp.broadcast_to(has_bottom, (C, 128)) == 1

    def column(parts):
        above, own, below = parts
        val = jnp.where((lane >= 1) & (lane <= ROWS), own, zero)
        val = jnp.where((lane == 0) & top_on, pltpu.roll(above, 64, 1), val)
        return jnp.where((lane == ROWS + 1) & bottom_on, pltpu.roll(below, 64, 1), val)

    cl, cr = column(left), column(right)
    for t in range(2 * PAIRS):
        base = grid[t // 2 + 1, t % 2]
        if t == 0:
            base = jnp.where((lane >= 1) & (lane <= COLS), jnp.where(top_on, row_top[...], zero), base)
        if t == 46:
            base = jnp.where(lane >= 93, jnp.where(bottom_on, row_bottom[0], zero), base)
        if t == 47:
            base = jnp.where(lane <= 54, jnp.where(bottom_on, row_bottom[1], zero), base)
        for l in range(128):
            r, c = divmod(t * 128 + l, PITCH)
            if r > ROWS + 1:
                continue
            if c == 0:
                base = jnp.where(lane == l, pltpu.roll(cl, (l - r) % 128, 1), base)
            if c == PITCH - 1:
                base = jnp.where(lane == l, pltpu.roll(cr, (l - r) % 128, 1), base)
        grid[t // 2 + 1, t % 2] = base


def shifted(grid, p, sign):
    lane = lax.broadcasted_iota(jnp.int32, (C, 128), 1)
    tiles = (grid[p, 1], grid[p + 1, 0], grid[p + 1, 1], grid[p + 2, 0])
    wins = []
    for a, b in TAPS:
        d = sign * (PITCH * (a - 1) + b - 1)
        if d == 0:
            wins.append(jnp.concatenate([tiles[1], tiles[2]], axis=1))
            continue
        base, s = (0, d + 128) if d < 0 else (1, d)
        rolled = [pltpu.roll(tiles[base + i], 128 - s, 1) for i in range(3)]
        keep = lane < 128 - s
        wins.append(jnp.concatenate(
            [jnp.where(keep, rolled[0], rolled[1]), jnp.where(keep, rolled[1], rolled[2])], axis=1))
    return wins


def kernel(sizes, x_ref, wf_ref, wb_ref, bias_ref, an_ref, fw_ref, gi_ref, gw_ref,
           pg, gg, stack, pred, mv, sc, an_t, acc, gi_t,
           row_top, row_bottom, edge, side,
           grow_top, grow_bottom, gedge, gside,
           ar0, ar1, ar2, a1, a2, ar3, ar4, ar5,
           hs, hr, gs, gr, fs, fr, bs, br,
           s1, r1, s2, r2, s3, r3, s4, r4, s5, r5):
    n_mem, n_lat, n_lon = sizes
    n_z, n_y = n_lon // 2, n_mem * 2
    mem, lat, lon = (lax.axis_index(a) for a in ("member", "lat", "lon"))
    z, y_lo = lon // 2, lax.rem(lon, 2)
    y = mem * 2 + y_lo

    def wrap(v, n):
        return lax.rem(v + n, n)

    def at_y(t):
        return {"member": t // 2, "lon": z * 2 + lax.rem(t, 2)}

    def at_z(t):
        return {"lon": t * 2 + y_lo}

    zeros12 = jnp.zeros((2, C - F, 128), BF)
    for p in range(PAIRS + 2):
        gg[p, :, F:C, :] = zeros12
    for grid in (pg, gg):
        grid[0] = jnp.zeros((2, C, 128), BF)
        grid[PAIRS + 1] = jnp.zeros((2, C, 128), BF)

    barrier = pltpu.get_barrier_semaphore()

    def greet(dev):
        pl.semaphore_signal(barrier, inc=1, device_id=dev, device_id_type=MESH)

    for j in range(1, n_lat):
        greet({"lat": wrap(lat + j, n_lat)})
    for j in range(1, n_z):
        greet(at_z(wrap(z + j, n_z)))
    for j in range(1, n_y):
        greet(at_y(wrap(y + j, n_y)))
    for dl in (-1, 0, 1):
        for dn in (-1, 1):
            greet({"lat": wrap(lat + dl, n_lat), "lon": wrap(lon + dn, n_lon)})
    greetings = n_lat - 1 + n_z - 1 + n_y - 1 + 6

    source = padded_source()

    def load_x(t):
        return x_ref[:, 128 * t:128 * t + 128]

    for t in range(2 * PAIRS):
        pg[t // 2 + 1, t % 2] = move_tile(source, t, load_x, C)
    first, last = edge_columns(pg)
    edge[0] = first
    edge[1] = last

    pl.semaphore_wait(barrier, greetings)

    def halo_copies(grid, edges, top, bottom, sides, send, recv):
        copies = [
            pltpu.make_async_remote_copy(
                grid.at[1], bottom, send.at[0], recv.at[0],
                device_id={"lat": wrap(lat - 1, n_lat)}, device_id_type=MESH),
            pltpu.make_async_remote_copy(
                grid.at[PAIRS, 0], top, send.at[1], recv.at[1],
                device_id={"lat": wrap(lat + 1, n_lat)}, device_id_type=MESH)]
        for dl in (-1, 0, 1):
            for which, dn in ((0, -1), (1, 1)):
                i = 2 + (dl + 1) * 2 + which
                copies.append(pltpu.make_async_remote_copy(
                    edges.at[which], sides.at[which, dl + 1], send.at[i], recv.at[i],
                    device_id={"lat": wrap(lat - dl, n_lat), "lon": wrap(lon + dn, n_lon)},
                    device_id_type=MESH))
        return copies

    halo = halo_copies(pg, edge, row_top, row_bottom, side, hs, hr)
    for copy in halo:
        copy.start()

    def load_an(t):
        return an_ref[:, 128 * t:128 * t + 128]

    for t in range(2 * PAIRS):
        an_t[t // 2, t % 2] = move_tile(source, t, load_an, F)
    ones = jnp.ones((STACK - 9 * C, 256), BF)
    for p in range(PAIRS):
        stack[p, 9 * C:STACK, :] = ones
    acc[...] = jnp.zeros_like(acc)

    for copy in halo:
        copy.wait()
    place_halo(pg, row_top, row_bottom, [side[1, i] for i in range(3)],
               [side[0, i] for i in range(3)], lat, n_lat)

    def out_copy(k, j):
        dest = wrap(mem + j, n_mem)
        return pltpu.make_async_remote_copy(
            pred.at[k * 4 + dest], mv.at[k, j - 1], fs.at[k, j - 1], fr.at[k, j - 1],
            device_id={"member": dest}, device_id_type=MESH)

    def back_copy(k, j):
        dest = wrap(mem - j, n_mem)
        return pltpu.make_async_remote_copy(
            sc.at[k, j - 1], gg.at[k * 4 + mem + 1, :, 0:F, :], bs.at[k, j - 1], br.at[k, j - 1],
            device_id={"member": dest}, device_id_type=MESH)

    bias = bias_ref[...]

    def forward(k, carry):
        def one(w, inner):
            p = k * 4 + w
            for i, win in enumerate(shifted(pg, p, 1)):
                stack[p, C * i:C * i + C, :] = win
            out = jnp.dot(wf_ref[...], stack[p], preferred_element_type=F32) + bias
            out = out.astype(BF)
            pred[p, 0] = out[:, :128]
            pred[p, 1] = out[:, 128:]
            return inner
        lax.fori_loop(0, 4, one, 0)
        for j in (2, 1, 3):
            out_copy(k, j).start()
        return carry

    lax.fori_loop(0, CHUNKS, forward, 0)

    fw = fw_ref[...][None]

    def score(k, carry):
        own = k * 4 + mem
        for j in (1, 3, 2):
            out_copy(k, j).wait_recv()
        vals = [pred[own].astype(F32)] + [mv[k, j].astype(F32) for j in range(3)]
        target = an_t[own].astype(F32)
        pair = [None] * 4
        for i in range(4):
            for j in range(i + 1, 4):
                s = slope(vals[i] - vals[j])
                pair[i] = s if pair[i] is None else pair[i] + s
                pair[j] = -s if pair[j] is None else pair[j] - s
        for i in range(4):
            s = fw * (slope(vals[i] - target) * 0.25 - pair[i] / 12.0)
            if i == 0:
                gg[own + 1, :, 0:F, :] = s.astype(BF)
            else:
                sc[k, i - 1] = s.astype(BF)
        for j in (2, 1, 3):
            back_copy(k, j).start()
        return carry

    lax.fori_loop(0, CHUNKS, score, 0)

    def weight_pair(p):
        g = jnp.concatenate([gg[p + 1, 0], gg[p + 1, 1]], axis=1)
        g = jnp.where(jnp.broadcast_to(interior(p), (C, 256)), g, jnp.zeros_like(g))
        acc[...] += lax.dot_general(g, stack[p], (((1,), (1,)), ((), ())), preferred_element_type=F32)

    def weights(k, carry):
        weight_pair(k * 4 + mem)
        for j in (1, 3, 2):
            pltpu.make_async_remote_copy(
                sc.at[k, j - 1], gg.at[k * 4 + wrap(mem + j, n_mem) + 1, :, 0:F, :],
                bs.at[k, j - 1], br.at[k, j - 1],
                device_id={"member": wrap(mem - j, n_mem)}, device_id_type=MESH).wait_recv()
            weight_pair(k * 4 + wrap(mem + j, n_mem))
        return carry

    lax.fori_loop(0, CHUNKS, weights, 0)

    for q in range(80):
        i, j = divmod(q, 7)
        ar0[q // 10, q % 10] = acc[8 * i:8 * i + 8, 128 * j:128 * j + 128] if q < 77 else jnp.zeros((8, 128), F32)

    def windows(t):
        return (t * 8) // 7

    def phase1(j):
        dest = wrap(lat + j, n_lat)
        return pltpu.make_async_remote_copy(
            ar0.at[dest], ar1.at[j - 1], s1.at[j - 1], r1.at[j - 1],
            device_id={"lat": dest}, device_id_type=MESH)

    def phase2(j):
        dest = wrap(z + j, n_z)
        return pltpu.make_async_remote_copy(
            a1.at[pl.ds(windows(dest), 2)], ar2.at[j - 1], s2.at[j - 1], r2.at[j - 1],
            device_id=at_z(dest), device_id_type=MESH)

    def phase3(j, slot):
        return pltpu.make_async_remote_copy(
            a2, ar3.at[slot], s3.at[j - 1], r3.at[slot],
            device_id=at_y(wrap(y + j, n_y)), device_id_type=MESH)

    def phase4(j, slot):
        return pltpu.make_async_remote_copy(
            ar4.at[z], ar4.at[slot], s4.at[j - 1], r4.at[slot],
            device_id=at_z(wrap(z + j, n_z)), device_id_type=MESH)

    def phase5(j, slot):
        return pltpu.make_async_remote_copy(
            ar5.at[lat], ar5.at[slot], s5.at[j - 1], r5.at[slot],
            device_id={"lat": wrap(lat + j, n_lat)}, device_id_type=MESH)

    for j in range(1, n_lat):
        phase1(j).start()

    first, last = edge_columns(gg)
    gedge[0] = first
    gedge[1] = last
    ghalo = halo_copies(gg, gedge, grow_top, grow_bottom, gside, gs, gr)
    for copy in ghalo:
        copy.start()

    for j in range(1, n_lat):
        phase1(j).wait_recv()
    total = ar0[lat]
    for j in range(n_lat - 1):
        total = total + ar1[j]
    a1[...] = total
    for j in range(1, n_z):
        phase2(j).start()

    for copy in ghalo:
        copy.wait()
    place_halo(gg, grow_top, grow_bottom, [gside[1, i] for i in range(3)],
               [gside[0, i] for i in range(3)], lat, n_lat)

    def back(p, carry):
        rhs = jnp.concatenate(shifted(gg, p, -1), axis=0)
        out = jnp.dot(wb_ref[...], rhs, preferred_element_type=F32).astype(BF)
        gi_t[p, 0] = out[:, :128]
        gi_t[p, 1] = out[:, 128:]
        return carry

    lax.fori_loop(0, 8, back, 0)
    for j in range(1, n_z):
        phase2(j).wait_recv()
    total = a1[pl.ds(windows(z), 2)]
    for j in range(n_z - 1):
        total = total + ar2[j]
    a2[...] = total
    ar3[y] = total
    for j in range(1, n_y):
        phase3(j, y).start()

    lax.fori_loop(8, 16, back, 0)
    for j in range(1, n_y):
        phase3(j, wrap(y + j, n_y)).wait_recv()
    total = ar3[0]
    for j in range(1, n_y):
        total = total + ar3[j]
    ar4[z] = total
    for j in range(1, n_z):
        phase4(j, z).start()

    lax.fori_loop(16, 24, back, 0)
    for j in range(1, n_z):
        phase4(j, wrap(z + j, n_z)).wait_recv()
    for i in range(10):
        owner = max(t for t in range(8) if (t * 8) // 7 <= i)
        ar5[lat, i] = ar4[owner, i - (owner * 8) // 7]
    for j in range(1, n_lat):
        phase5(j, lat).start()

    dense = dense_source()

    def load_gi(t):
        return gi_t[t // 2, t % 2]

    for t in range(CELLS // 128):
        gi_ref[:, 128 * t:128 * t + 128] = move_tile(dense, t, load_gi, C)

    for j in range(1, n_lat):
        phase5(j, wrap(lat + j, n_lat)).wait_recv()
    for q in range(77):
        i, j = divmod(q, 7)
        gw_ref[8 * i:8 * i + 8, 128 * j:128 * j + 128] = ar5[q // 10, q % 10]

    def sent(k, carry):
        for j in (1, 2, 3):
            out_copy(k, j).wait_send()
            back_copy(k, j).wait_send()
        return carry

    lax.fori_loop(0, CHUNKS, sent, 0)
    for j in range(1, n_lat):
        phase1(j).wait_send()
        phase5(j, lat).wait_send()
    for j in range(1, n_z):
        phase2(j).wait_send()
        phase4(j, z).wait_send()
    for j in range(1, n_y):
        phase3(j, y).wait_send()


def solution(mesh):
    sizes = tuple(mesh.shape[a] for a in ("member", "lat", "lon"))

    def local(inputs, weight, bias, analysis, field_weight):
        x = inputs[0, :, 0, 0]
        target = analysis[:, 0, 0]
        taps = weight.reshape(9, C, F)
        wf = jnp.pad(taps.transpose(2, 0, 1).reshape(F, 9 * C), ((0, 0), (0, STACK - 9 * C)))
        wb = jnp.pad(taps, ((0, 0), (0, 0), (0, C - F))).transpose(1, 0, 2).reshape(C, 9 * C)
        vm = pltpu.VMEM
        dma = pltpu.SemaphoreType.DMA
        scratch = [
            vm((PAIRS + 2, 2, C, 128), BF),
            vm((PAIRS + 2, 2, C, 128), BF),
            vm((PAIRS, STACK, 256), BF),
            vm((PAIRS, 2, F, 128), BF),
            vm((CHUNKS, 3, 2, F, 128), BF),
            vm((CHUNKS, 3, 2, F, 128), BF),
            vm((PAIRS, 2, F, 128), BF),
            vm((C, STACK), F32),
            vm((PAIRS, 2, C, 128), BF),
            vm((C, 128), BF), vm((2, C, 128), BF), vm((2, C, 128), BF), vm((2, 3, C, 128), BF),
            vm((C, 128), BF), vm((2, C, 128), BF), vm((2, C, 128), BF), vm((2, 3, C, 128), BF),
            vm((8, 10, 8, 128), F32),
            vm((7, 10, 8, 128), F32),
            vm((7, 2, 8, 128), F32),
            vm((10, 8, 128), F32),
            vm((2, 8, 128), F32),
            vm((8, 2, 8, 128), F32),
            vm((8, 2, 8, 128), F32),
            vm((8, 10, 8, 128), F32),
            dma((8,)), dma((8,)), dma((8,)), dma((8,)),
            dma((CHUNKS, 3)), dma((CHUNKS, 3)), dma((CHUNKS, 3)), dma((CHUNKS, 3)),
            dma((7,)), dma((7,)), dma((7,)), dma((7,)), dma((7,)), dma((8,)),
            dma((7,)), dma((8,)), dma((7,)), dma((8,)),
        ]

        def body(*refs):
            kernel(sizes, *refs)

        gi, gw = pl.pallas_call(
            body,
            out_shape=(jax.ShapeDtypeStruct((C, CELLS), BF), jax.ShapeDtypeStruct((88, STACK), F32)),
            in_specs=[pl.BlockSpec(memory_space=vm)] * 6,
            out_specs=[pl.BlockSpec(memory_space=vm)] * 2,
            scratch_shapes=scratch,
            compiler_params=pltpu.CompilerParams(
                collective_id=0, has_side_effects=True, vmem_limit_bytes=56 * 2**20),
        )(x, wf, wb, bias[:, None], target, field_weight[:, None])
        cells = CELLS * sizes[1] * sizes[2]
        gw = gw[:F] / cells
        grad_weight = gw[:, :9 * C].reshape(F, 9, C).transpose(1, 2, 0).reshape(9, C * F)
        return gi.reshape(1, C, 1, 1, CELLS), grad_weight, gw[:, 9 * C]

    placed = (P("member", None, "lat", "lon", None), P(), P(), P(None, "lat", "lon", None), P())
    return jax.shard_map(
        local,
        mesh=mesh,
        in_specs=placed,
        out_specs=(P("member", None, "lat", "lon", None), P(), P()),
        check_vma=False,
    )
```

```python
import numpy as np
import jax
import jax.numpy as jnp
from jax import lax
from jax.experimental import pallas as pl
from jax.experimental.pallas import tpu as pltpu
from jax.sharding import PartitionSpec as P

MESH = pl.DeviceIdType.MESH
C, F, ROWS, COLS = 96, 84, 64, 90
CELLS = ROWS * COLS
PITCH = COLS + 2
PAIRS = 24
CHUNKS = 6
STACK = 896
EARLY = 3
BACK = (3, 6, 9)
BF, F32 = jnp.bfloat16, jnp.float32
TAPS = [(a, b) for a in range(3) for b in range(3)]


def padded_source():
    lane = np.arange(PAIRS * 256)
    r, c = lane // PITCH, lane % PITCH
    inside = (r >= 1) & (r <= ROWS) & (c >= 1) & (c <= COLS)
    return np.where(inside, COLS * (r - 1) + c - 1, -1)


def dense_source():
    cell = np.arange(CELLS)
    return PITCH * (cell // COLS + 1) + cell % COLS + 1


def segments(source, tile):
    out = []
    for lane in range(128):
        src = source[tile * 128 + lane]
        key = (None, 0) if src < 0 else (int(src) // 128, int(lane - src) % 128)
        if not out or out[-1][1:] != key:
            out.append((lane,) + key)
    return out


def move_tile(source, tile, load, rows):
    lane = lax.broadcasted_iota(jnp.int32, (rows, 128), 1)
    acc = None
    for first, src, shift in segments(source, tile):
        if src is None:
            val = jnp.zeros((rows, 128), BF)
        else:
            val = load(src)
            if shift:
                val = pltpu.roll(val, shift, 1)
        acc = val if acc is None else jnp.where(lane >= first, val, acc)
    return acc


def lane_grid(p):
    o = p * 256 + lax.broadcasted_iota(jnp.int32, (1, 256), 1)
    r = lax.shift_right_logical(o * 45591, 22)
    c = o - r * PITCH
    return r, c


def interior(p):
    r, c = lane_grid(p)
    return (r >= 1) & (r <= ROWS) & (c >= 1) & (c <= COLS)


def slope(u):
    return u * lax.rsqrt(u * u + 1.0)


def edge_columns(grid, edges, rows):
    lane = lax.broadcasted_iota(jnp.int32, (C, 128), 1)
    found = [edges[0], edges[1]]
    for r in rows:
        for which, col in enumerate((1, COLS)):
            o = PITCH * r + col
            t, l = o // 128, o % 128
            val = grid[t // 2 + 1, t % 2]
            val = pltpu.roll(val, (r - l) % 128, 1)
            found[which] = jnp.where(lane == r, val, found[which])
    edges[0] = found[0]
    edges[1] = found[1]


def rows_of_chunk(k):
    return [r for r in range(1, ROWS + 1) if (PITCH * r + COLS) // (256 * 4) == k]


def place_halo(grid, arrived, lat, n_lat):
    lane = lax.broadcasted_iota(jnp.int32, (C, 128), 1)
    zero = jnp.zeros((C, 128), BF)
    has_top = jnp.where(lat > 0, 1, 0)
    has_bottom = jnp.where(lat < n_lat - 1, 1, 0)
    top_on = jnp.broadcast_to(has_top, (C, 128)) == 1
    bottom_on = jnp.broadcast_to(has_bottom, (C, 128)) == 1

    def column(at):
        above, own, below = (arrived[at + i] for i in range(3))
        val = jnp.where((lane >= 1) & (lane <= ROWS), own, zero)
        val = jnp.where((lane == 0) & top_on, pltpu.roll(above, 64, 1), val)
        return jnp.where((lane == ROWS + 1) & bottom_on, pltpu.roll(below, 64, 1), val)

    cl, cr = column(6), column(3)
    for t in range(2 * PAIRS):
        base = grid[t // 2 + 1, t % 2]
        if t == 0:
            base = jnp.where((lane >= 1) & (lane <= COLS), jnp.where(top_on, arrived[0], zero), base)
        if t == 46:
            base = jnp.where(lane >= 93, jnp.where(bottom_on, arrived[1], zero), base)
        if t == 47:
            base = jnp.where(lane <= 54, jnp.where(bottom_on, arrived[2], zero), base)
        for l in range(128):
            r, c = divmod(t * 128 + l, PITCH)
            if r > ROWS + 1:
                continue
            if c == 0:
                base = jnp.where(lane == l, pltpu.roll(cl, (l - r) % 128, 1), base)
            if c == PITCH - 1:
                base = jnp.where(lane == l, pltpu.roll(cr, (l - r) % 128, 1), base)
        grid[t // 2 + 1, t % 2] = base


def fill_stack(grid, p, sign, dst):
    lane = lax.broadcasted_iota(jnp.int32, (C, 128), 1)
    tiles = (grid[p, 1], grid[p + 1, 0], grid[p + 1, 1], grid[p + 2, 0], grid[p + 2, 1], grid[p + 3, 0])
    for i, (a, b) in enumerate(TAPS):
        d = sign * (PITCH * (a - 1) + b - 1)
        if d == 0:
            win = tiles[1:5]
        else:
            base, s = (0, d + 128) if d < 0 else (1, d)
            rolled = [pltpu.roll(tiles[base + n], 128 - s, 1) for n in range(5)]
            keep = lane < 128 - s
            win = [jnp.where(keep, rolled[n], rolled[n + 1]) for n in range(4)]
        for n in range(4):
            dst(n // 2)[C * i:C * i + C, 128 * (n % 2):128 * (n % 2) + 128] = win[n]


def kernel(sizes, x_hbm, an_hbm, w_hbm, bias_hbm, fw_hbm, gi_hbm, gw_ref, gb_ref,
           x_ref, an_ref, gi_ref, w_ref, bias_ref, fw_ref, wrows, picked, wf, wb, full,
           pg, gg, stack, bstack, pred, mv, sc, an_t, acc, gi_t,
           edge, arrived, gedge, garrived,
           ar0, ar1, ar2, a1, a2, ar3, ar4, ar5,
           pace, io, hs, hr, gs, gr, fs, fr, bs, br,
           s1, r1, s2, r2, s3, r3, s4, r4, s5, r5):
    n_mem, n_lat, n_lon = sizes
    n_z, n_y = n_lon // 2, n_mem * 2
    mem, lat, lon = (lax.axis_index(a) for a in ("member", "lat", "lon"))
    z, y_lo = lon // 2, lax.rem(lon, 2)
    y = mem * 2 + y_lo

    load_x = pltpu.make_async_copy(x_hbm, x_ref, io.at[0])
    load_an = pltpu.make_async_copy(an_hbm, an_ref, io.at[1])
    loads = [pltpu.make_async_copy(src, dst, io.at[3 + i]) for i, (src, dst) in enumerate(
        ((w_hbm, w_ref), (bias_hbm, bias_ref), (fw_hbm, fw_ref)))]
    load_x.start()
    for copy in loads:
        copy.start()
    load_an.start()

    def wrap(v, n):
        return lax.rem(v + n, n)

    def at_y(t):
        return {"member": t // 2, "lon": z * 2 + lax.rem(t, 2)}

    def at_z(t):
        return {"lon": t * 2 + y_lo}

    zeros12 = jnp.zeros((2, C - F, 128), BF)
    for p in range(PAIRS + 2):
        gg[p, :, F:C, :] = zeros12
    for p in (0, PAIRS + 1):
        gg[p, :, 0:F, :] = jnp.zeros((2, F, 128), BF)

    barrier = pltpu.get_barrier_semaphore()

    def greet(dev):
        pl.semaphore_signal(barrier, inc=1, device_id=dev, device_id_type=MESH)

    for dl in (-1, 0, 1):
        for dn in (-1, 1):
            greet({"lat": wrap(lat + dl, n_lat), "lon": wrap(lon + dn, n_lon)})
    for j in range(1, n_lat):
        greet({"lat": wrap(lat + j, n_lat)})
    for j in range(1, n_z):
        greet(at_z(wrap(z + j, n_z)))
    for j in range(1, n_y):
        greet(at_y(wrap(y + j, n_y)))
    greetings = n_lat - 1 + n_z - 1 + n_y - 1 + 6

    source = padded_source()
    for p in (0, PAIRS + 1):
        pg[p] = jnp.zeros((2, C, 128), BF)
    edge[...] = jnp.zeros_like(edge)
    load_x.wait()
    for t in range(2 * PAIRS):
        pg[t // 2 + 1, t % 2] = move_tile(source, t, lambda i: x_ref[:, 128 * i:128 * i + 128], C)
    edge_columns(pg, edge, range(1, ROWS + 1))

    pl.semaphore_wait(barrier, greetings)

    def landed(ref, sem):
        pltpu.make_async_copy(ref, ref, sem).wait()

    def halo_copies(grid, edges, into, send, recv):
        copies = []
        for dl in (-1, 1, 0):
            for which, dn in ((0, -1), (1, 1)):
                copies.append(pltpu.make_async_remote_copy(
                    edges.at[which], into.at[3 + 3 * which + dl + 1], send, recv,
                    device_id={"lat": wrap(lat - dl, n_lat), "lon": wrap(lon + dn, n_lon)},
                    device_id_type=MESH))
        copies += [
            pltpu.make_async_remote_copy(
                grid.at[1], into.at[1:3], send, recv,
                device_id={"lat": wrap(lat - 1, n_lat)}, device_id_type=MESH),
            pltpu.make_async_remote_copy(
                grid.at[PAIRS, 0], into.at[0], send, recv,
                device_id={"lat": wrap(lat + 1, n_lat)}, device_id_type=MESH)]
        return copies

    halo = halo_copies(pg, edge, arrived, hs, hr)
    for copy in halo:
        copy.start()

    for copy in loads:
        copy.wait()
    wf[:, 9 * C:STACK] = jnp.zeros((F, STACK - 9 * C), BF)
    wb[...] = jnp.zeros_like(wb)
    strips = C * F // 128
    for i in range(strips):
        wrows[16 * i:16 * i + 9, :] = w_ref[:, 128 * i:128 * i + 128].astype(F32)
    channel = lax.broadcasted_iota(jnp.int32, (C, strips), 0)
    strip = lax.broadcasted_iota(jnp.int32, (C, strips), 1)
    begin = lax.shift_right_logical(channel * F, 7)
    pick = jnp.concatenate(
        [jnp.where(strip == begin + n, 1.0, 0.0).astype(BF) for n in range(2)], axis=0)
    strip_rows = jnp.concatenate(
        [wrows[pl.ds(i, strips, stride=16), :].astype(BF) for i in range(9)], axis=1)
    picked[...] = jnp.dot(pick, strip_rows, preferred_element_type=F32)
    offset = (lax.broadcasted_iota(jnp.int32, (C, 128), 0) * F) & 127
    from_first = lax.broadcasted_iota(jnp.int32, (C, 128), 1) >= offset
    for i in range(9):
        tap = jnp.where(from_first, picked[0:C, 128 * i:128 * i + 128],
                        picked[C:2 * C, 128 * i:128 * i + 128])
        for bit in (4, 8, 16, 32, 64):
            tap = jnp.where((offset & bit) != 0, pltpu.roll(tap, 128 - bit, 1), tap)
        tap = tap[:, :F]
        wb[:, C * i:C * i + F] = tap.astype(BF)
        wf[:, C * i:C * i + C] = tap.T.astype(BF)

    def as_column(row):
        square = lax.broadcasted_iota(jnp.int32, (F, F), 0) == lax.broadcasted_iota(jnp.int32, (F, F), 1)
        return jnp.sum(jnp.where(square, jnp.broadcast_to(row, (F, F)), 0.0), axis=1, keepdims=True)

    bias = as_column(bias_ref[...])
    fw = as_column(fw_ref[...])[None]

    acc[...] = jnp.zeros_like(acc)
    gedge[...] = jnp.zeros_like(gedge)
    load_an.wait()
    for t in range(2 * PAIRS):
        an_t[t // 2, t % 2] = move_tile(source, t, lambda i: an_ref[:, 128 * i:128 * i + 128], F)
    ones = jnp.ones((STACK - 9 * C, 256), BF)
    for p in range(PAIRS):
        stack[p, 9 * C:STACK, :] = ones

    landed(arrived, hr)
    landed(arrived, hs)
    place_halo(pg, arrived, lat, n_lat)

    def out_copy(k, j):
        dest = wrap(mem + j, n_mem)
        return pltpu.make_async_remote_copy(
            pred.at[k * 4 + dest], mv.at[k, j - 1], fs.at[k, j - 1], fr.at[k, j - 1],
            device_id={"member": dest}, device_id_type=MESH)

    def back_copy(k, j):
        dest = wrap(mem - j, n_mem)
        return pltpu.make_async_remote_copy(
            sc.at[k, j - 1], gg.at[k * 4 + mem + 1, :, 0:F, :], bs.at[k, j - 1], br.at[k, j - 1],
            device_id={"member": dest}, device_id_type=MESH)

    def back_arrival(k, j):
        return pltpu.make_async_remote_copy(
            sc.at[k, j - 1], gg.at[k * 4 + wrap(mem + j, n_mem) + 1, :, 0:F, :],
            bs.at[k, j - 1], br.at[k, j - 1],
            device_id={"member": wrap(mem - j, n_mem)}, device_id_type=MESH)

    def forward(k):
        def one(h, inner):
            p = k * 4 + 2 * h
            fill_stack(pg, p, 1, lambda n: stack.at[p + n])
            for n in range(2):
                out = jnp.dot(wf[...], stack[p + n], preferred_element_type=F32) + bias
                out = out.astype(BF)
                pred[p + n, 0] = out[:, :128]
                pred[p + n, 1] = out[:, 128:]
            return inner
        lax.fori_loop(0, 2, one, 0)
        for j in (2, 1, 3):
            out_copy(k, j).start()

    def score(k):
        own = k * 4 + mem
        for j in (1, 3, 2):
            out_copy(k, j).wait_recv()
        vals = [pred[own].astype(F32)] + [mv[k, j].astype(F32) for j in range(3)]
        target = an_t[own].astype(F32)
        pair = [None] * 4
        for i in range(4):
            for j in range(i + 1, 4):
                s = slope(vals[i] - vals[j])
                pair[i] = s if pair[i] is None else pair[i] + s
                pair[j] = -s if pair[j] is None else pair[j] - s
        for i in (2, 1, 3, 0):
            s = fw * (slope(vals[i] - target) * 0.25 - pair[i] / 12.0)
            if i == 0:
                gg[own + 1, :, 0:F, :] = s.astype(BF)
            else:
                sc[k, i - 1] = s.astype(BF)

    def send_back(k):
        for j in (2, 1, 3):
            back_copy(k, j).start()

    def weight_pair(p):
        g = jnp.concatenate([gg[p + 1, 0], gg[p + 1, 1]], axis=1)
        g = jnp.where(jnp.broadcast_to(interior(p), (C, 256)), g, jnp.zeros_like(g))
        acc[...] += lax.dot_general(g, stack[p], (((1,), (1,)), ((), ())), preferred_element_type=F32)

    ghalo = halo_copies(gg, gedge, garrived, gs, gr)

    def weights(k):
        weight_pair(k * 4 + mem)
        for j in (1, 3):
            back_arrival(k, j).wait_recv()
            weight_pair(k * 4 + wrap(mem + j, n_mem))
        back_arrival(k, 2).wait_recv()
        for chunk in range(CHUNKS):
            @pl.when(k == chunk)
            def _():
                edge_columns(gg, gedge, rows_of_chunk(chunk))
                if chunk == CHUNKS - 1:
                    for copy in ghalo:
                        copy.start()
        weight_pair(k * 4 + wrap(mem + 2, n_mem))

    def each(first, last, step):
        def run(k, carry):
            step(k)
            return carry
        lax.fori_loop(first, last, run, 0)

    each(0, CHUNKS, forward)
    each(0, EARLY, score)
    other_lat = lat + 1 - 2 * lax.rem(lat, 2)
    other_lon = z * 2 + 1 - y_lo
    for dev in ({"lat": other_lat}, {"lon": other_lon}, {"lat": other_lat, "lon": other_lon}):
        pl.semaphore_signal(pace, inc=1, device_id=dev, device_id_type=MESH)
    pl.semaphore_wait(pace, 3)
    each(0, EARLY, send_back)

    def late(k):
        score(k)
        send_back(k)

    each(EARLY, CHUNKS, late)
    each(0, CHUNKS, weights)

    for q in range(80):
        i, j = divmod(q, 7)
        ar0[q // 10, q % 10] = acc[8 * i:8 * i + 8, 128 * j:128 * j + 128] if q < 77 else jnp.zeros((8, 128), F32)

    def windows(t):
        return (t * 8) // 7

    def phase1(j):
        dest = wrap(lat + j, n_lat)
        return pltpu.make_async_remote_copy(
            ar0.at[dest], ar1.at[j - 1], s1, r1,
            device_id={"lat": dest}, device_id_type=MESH)

    def phase2(j):
        dest = wrap(z + j, n_z)
        return pltpu.make_async_remote_copy(
            a1.at[pl.ds(windows(dest), 2)], ar2.at[j - 1], s2, r2,
            device_id=at_z(dest), device_id_type=MESH)

    def phase3(j, slot):
        return pltpu.make_async_remote_copy(
            a2, ar3.at[slot], s3, r3,
            device_id=at_y(wrap(y + j, n_y)), device_id_type=MESH)

    def phase4(j, slot):
        return pltpu.make_async_remote_copy(
            ar4.at[z], ar4.at[slot], s4, r4,
            device_id=at_z(wrap(z + j, n_z)), device_id_type=MESH)

    def phase5(j, slot):
        return pltpu.make_async_remote_copy(
            ar5.at[lat], ar5.at[slot], s5, r5,
            device_id={"lat": wrap(lat + j, n_lat)}, device_id_type=MESH)

    far_first = (4, 3, 5, 2, 6, 1, 7)
    for j in far_first:
        phase1(j).start()

    def back(h, carry):
        p = 2 * h
        fill_stack(gg, p, -1, lambda n: bstack.at[n])
        for n in range(2):
            out = jnp.dot(wb[...], bstack[n], preferred_element_type=F32).astype(BF)
            gi_t[p + n, 0] = out[:, :128]
            gi_t[p + n, 1] = out[:, 128:]
        return carry

    landed(ar1, r1)
    total = ar0[lat]
    for j in range(n_lat - 1):
        total = total + ar1[j]
    a1[...] = total
    for j in far_first:
        phase2(j).start()

    landed(garrived, gr)
    landed(garrived, gs)
    place_halo(gg, garrived, lat, n_lat)

    lax.fori_loop(0, BACK[0], back, 0)
    landed(ar2, r2)
    total = a1[pl.ds(windows(z), 2)]
    for j in range(n_z - 1):
        total = total + ar2[j]
    a2[...] = total
    ar3[y] = total
    for j in far_first:
        phase3(j, y).start()

    lax.fori_loop(BACK[0], BACK[1], back, 0)
    landed(ar3.at[0:7], r3)
    total = ar3[0]
    for j in range(1, n_y):
        total = total + ar3[j]
    ar4[z] = total
    for j in far_first:
        phase4(j, z).start()

    lax.fori_loop(BACK[1], BACK[2], back, 0)
    landed(ar4.at[0:7], r4)
    for i in range(10):
        owner = max(t for t in range(8) if (t * 8) // 7 <= i)
        ar5[lat, i] = ar4[owner, i - (owner * 8) // 7]
    for j in far_first:
        phase5(j, lat).start()

    lax.fori_loop(BACK[2], PAIRS // 2, back, 0)
    dense = dense_source()
    for t in range(CELLS // 128):
        gi_ref[:, 128 * t:128 * t + 128] = move_tile(dense, t, lambda i: gi_t[i // 2, i % 2], C)
    store_gi = pltpu.make_async_copy(gi_ref, gi_hbm, io.at[2])
    store_gi.start()

    def sent(k):
        for j in (1, 2, 3):
            out_copy(k, j).wait_send()
            back_copy(k, j).wait_send()

    each(0, CHUNKS, sent)
    landed(ar1, s1)
    landed(ar2, s2)
    landed(ar2, s3)
    landed(ar2, s4)
    landed(ar5.at[0:7], r5)
    scale = 1.0 / (CELLS * n_lat * n_lon)
    for q in range(77):
        i, j = divmod(q, 7)
        full[8 * i:8 * i + 8, 128 * j:128 * j + 128] = ar5[q // 10, q % 10] * scale
    for j in range(7):
        turned = full[:, 128 * j:128 * j + 128].T
        if j < 6:
            gw_ref[128 * j:128 * j + 128, :] = turned[:, :F]
        else:
            gw_ref[128 * j:9 * C, :] = turned[:9 * C - 128 * j, :F]
            gb_ref[...] = turned[9 * C - 128 * j:9 * C - 128 * j + 1, :F]
    landed(ar1, s5)
    store_gi.wait()


def solution(mesh):
    sizes = tuple(mesh.shape[a] for a in ("member", "lat", "lon"))

    def local(inputs, weight, bias, analysis, field_weight):
        x = inputs[0, :, 0, 0]
        target = analysis[:, 0, 0]
        vm = pltpu.VMEM
        dma = pltpu.SemaphoreType.DMA
        halo = [vm((2, C, 128), BF), vm((9, C, 128), BF)]
        scratch = [
            vm((C, CELLS), BF),
            vm((F, CELLS), BF),
            vm((C, CELLS), BF),
            vm((9, C * F), BF),
            vm((1, F), F32),
            vm((1, F), F32),
            vm((16 * (C * F // 128), 128), F32),
            vm((2 * C, 9 * 128), F32),
            vm((F, STACK), BF),
            vm((C, 9 * C), BF),
            vm((C, STACK), F32),
            vm((PAIRS + 2, 2, C, 128), BF),
            vm((PAIRS + 2, 2, C, 128), BF),
            vm((PAIRS, STACK, 256), BF),
            vm((2, 9 * C, 256), BF),
            vm((PAIRS, 2, F, 128), BF),
            vm((CHUNKS, 3, 2, F, 128), BF),
            vm((CHUNKS, 3, 2, F, 128), BF),
            vm((PAIRS, 2, F, 128), BF),
            vm((C, STACK), F32),
            vm((PAIRS, 2, C, 128), BF),
            *halo, *halo,
            vm((8, 10, 8, 128), F32),
            vm((7, 10, 8, 128), F32),
            vm((7, 2, 8, 128), F32),
            vm((10, 8, 128), F32),
            vm((2, 8, 128), F32),
            vm((8, 2, 8, 128), F32),
            vm((8, 2, 8, 128), F32),
            vm((8, 10, 8, 128), F32),
            pltpu.SemaphoreType.REGULAR,
            dma((6,)), dma, dma, dma, dma,
            *[dma((CHUNKS, 3))] * 4,
            *[dma] * 10,
        ]

        def body(*refs):
            kernel(sizes, *refs)

        here, far = pl.BlockSpec(memory_space=vm), pl.BlockSpec(memory_space=pl.ANY)
        gi, gw, gb = pl.pallas_call(
            body,
            out_shape=(jax.ShapeDtypeStruct((C, CELLS), BF), jax.ShapeDtypeStruct((9 * C, F), F32),
                       jax.ShapeDtypeStruct((1, F), F32)),
            in_specs=[far] * 5,
            out_specs=[far, here, here],
            scratch_shapes=scratch,
            compiler_params=pltpu.CompilerParams(
                collective_id=0, has_side_effects=True, vmem_limit_bytes=32 * 2**20),
        )(x, target, weight, bias[None], field_weight[None])
        return gi.reshape(1, C, 1, 1, CELLS), gw.reshape(9, C * F), gb[0]

    placed = (P("member", None, "lat", "lon", None), P(), P(), P(None, "lat", "lon", None), P())
    return jax.shard_map(
        local,
        mesh=mesh,
        in_specs=placed,
        out_specs=(P("member", None, "lat", "lon", None), P(), P()),
        check_vma=False,
    )
```

```python
import numpy as np
import jax
import jax.numpy as jnp
from jax import lax
from jax.experimental import pallas as pl
from jax.experimental.pallas import tpu as pltpu
from jax.sharding import PartitionSpec as P

MESH = pl.DeviceIdType.MESH
C, F, ROWS, COLS = 96, 84, 64, 90
CELLS = ROWS * COLS
PITCH = COLS + 2
PAIRS = 24
CHUNKS = 6
STACK = 896
EARLY = 2
BACK = (3, 6, 9)
BF, F32 = jnp.bfloat16, jnp.float32
TAPS = [(a, b) for a in range(3) for b in range(3)]


def padded_source():
    lane = np.arange(PAIRS * 256)
    r, c = lane // PITCH, lane % PITCH
    inside = (r >= 1) & (r <= ROWS) & (c >= 1) & (c <= COLS)
    return np.where(inside, COLS * (r - 1) + c - 1, -1)


def dense_source():
    cell = np.arange(CELLS)
    return PITCH * (cell // COLS + 1) + cell % COLS + 1


def segments(source, tile):
    out = []
    for lane in range(128):
        src = source[tile * 128 + lane]
        key = (None, 0) if src < 0 else (int(src) // 128, int(lane - src) % 128)
        if not out or out[-1][1:] != key:
            out.append((lane,) + key)
    return out


def move_tile(source, tile, load, rows):
    lane = lax.broadcasted_iota(jnp.int32, (rows, 128), 1)
    acc = None
    for first, src, shift in segments(source, tile):
        if src is None:
            val = jnp.zeros((rows, 128), BF)
        else:
            val = load(src)
            if shift:
                val = pltpu.roll(val, shift, 1)
        acc = val if acc is None else jnp.where(lane >= first, val, acc)
    return acc


def lane_grid(p):
    o = p * 256 + lax.broadcasted_iota(jnp.int32, (1, 256), 1)
    r = lax.shift_right_logical(o * 45591, 22)
    c = o - r * PITCH
    return r, c


def interior(p):
    r, c = lane_grid(p)
    return (r >= 1) & (r <= ROWS) & (c >= 1) & (c <= COLS)


def slope(u):
    return u * lax.rsqrt(u * u + 1.0)


def edge_columns(grid, edges, rows):
    lane = lax.broadcasted_iota(jnp.int32, (C, 128), 1)
    found = [edges[0], edges[1]]
    for r in rows:
        for which, col in enumerate((1, COLS)):
            o = PITCH * r + col
            t, l = o // 128, o % 128
            val = grid[t // 2 + 1, t % 2]
            val = pltpu.roll(val, (r - l) % 128, 1)
            found[which] = jnp.where(lane == r, val, found[which])
    edges[0] = found[0]
    edges[1] = found[1]


def rows_of_chunk(k):
    return [r for r in range(1, ROWS + 1) if (PITCH * r + COLS) // (256 * 4) == k]


def place_halo(grid, arrived, lat, n_lat, tiles=range(2 * PAIRS)):
    lane = lax.broadcasted_iota(jnp.int32, (C, 128), 1)
    zero = jnp.zeros((C, 128), BF)
    has_top = jnp.where(lat > 0, 1, 0)
    has_bottom = jnp.where(lat < n_lat - 1, 1, 0)
    top_on = jnp.broadcast_to(has_top, (C, 128)) == 1
    bottom_on = jnp.broadcast_to(has_bottom, (C, 128)) == 1

    def column(at):
        above, own, below = (arrived[at + i] for i in range(3))
        val = jnp.where((lane >= 1) & (lane <= ROWS), own, zero)
        val = jnp.where((lane == 0) & top_on, pltpu.roll(above, 64, 1), val)
        return jnp.where((lane == ROWS + 1) & bottom_on, pltpu.roll(below, 64, 1), val)

    cl, cr = column(6), column(3)
    for t in tiles:
        base = grid[t // 2 + 1, t % 2]
        if t == 0:
            base = jnp.where((lane >= 1) & (lane <= COLS), jnp.where(top_on, arrived[0], zero), base)
        if t == 46:
            base = jnp.where(lane >= 93, jnp.where(bottom_on, arrived[1], zero), base)
        if t == 47:
            base = jnp.where(lane <= 54, jnp.where(bottom_on, arrived[2], zero), base)
        for l in range(128):
            r, c = divmod(t * 128 + l, PITCH)
            if r > ROWS + 1:
                continue
            if c == 0:
                base = jnp.where(lane == l, pltpu.roll(cl, (l - r) % 128, 1), base)
            if c == PITCH - 1:
                base = jnp.where(lane == l, pltpu.roll(cr, (l - r) % 128, 1), base)
        grid[t // 2 + 1, t % 2] = base


def fill_stack(grid, p, sign, dst):
    lane = lax.broadcasted_iota(jnp.int32, (C, 128), 1)
    tiles = (grid[p, 1], grid[p + 1, 0], grid[p + 1, 1], grid[p + 2, 0], grid[p + 2, 1], grid[p + 3, 0])
    for i, (a, b) in enumerate(TAPS):
        d = sign * (PITCH * (a - 1) + b - 1)
        if d == 0:
            win = tiles[1:5]
        else:
            base, s = (0, d + 128) if d < 0 else (1, d)
            rolled = [pltpu.roll(tiles[base + n], 128 - s, 1) for n in range(5)]
            keep = lane < 128 - s
            win = [jnp.where(keep, rolled[n], rolled[n + 1]) for n in range(4)]
        for n in range(4):
            dst(n // 2)[C * i:C * i + C, 128 * (n % 2):128 * (n % 2) + 128] = win[n]


def kernel(sizes, x_hbm, an_hbm, w_hbm, bias_hbm, fw_hbm, gi_hbm, gw_hbm, gb_hbm,
           x_ref, an_ref, gi_ref, gw_ref, gb_ref, w_ref, bias_ref, fw_ref, wrows, picked, wf, wb, full,
           pg, gg, stack, bstack, pred, mv, sc, an_t, acc, gi_t,
           edge, arrived, gedge, garrived,
           ar0, ar1, ar2, a1, a2, ar3, ar4, ar5,
           pace, io, hs, hr, gs, gr, fs, fr, bs, br,
           s1, r1, s2, r2, s3, r3, s4, r4, s5, r5):
    n_mem, n_lat, n_lon = sizes
    n_z, n_y = n_lon // 2, n_mem * 2
    mem, lat, lon = (lax.axis_index(a) for a in ("member", "lat", "lon"))
    z, y_lo = lon // 2, lax.rem(lon, 2)
    y = mem * 2 + y_lo

    load_x = pltpu.make_async_copy(x_hbm, x_ref, io.at[0])
    load_an = pltpu.make_async_copy(an_hbm, an_ref, io.at[1])
    loads = [pltpu.make_async_copy(src, dst, io.at[3 + i]) for i, (src, dst) in enumerate(
        ((w_hbm, w_ref), (bias_hbm, bias_ref), (fw_hbm, fw_ref)))]
    load_x.start()
    for copy in loads:
        copy.start()
    load_an.start()

    def wrap(v, n):
        return lax.rem(v + n, n)

    def at_y(t):
        return {"member": t // 2, "lon": z * 2 + lax.rem(t, 2)}

    def at_z(t):
        return {"lon": t * 2 + y_lo}

    zeros12 = jnp.zeros((2, C - F, 128), BF)
    for p in range(PAIRS + 2):
        gg[p, :, F:C, :] = zeros12
    for p in (0, PAIRS + 1):
        gg[p, :, 0:F, :] = jnp.zeros((2, F, 128), BF)

    barrier = pltpu.get_barrier_semaphore()

    def greet(dev):
        pl.semaphore_signal(barrier, inc=1, device_id=dev, device_id_type=MESH)

    for dl in (-1, 0, 1):
        for dn in (-1, 1):
            greet({"lat": wrap(lat + dl, n_lat), "lon": wrap(lon + dn, n_lon)})
    for j in range(1, n_lat):
        greet({"lat": wrap(lat + j, n_lat)})
    for j in range(1, n_z):
        greet(at_z(wrap(z + j, n_z)))
    for j in range(1, n_y):
        greet(at_y(wrap(y + j, n_y)))
    greetings = n_lat - 1 + n_z - 1 + n_y - 1 + 6

    source = padded_source()
    for p in (0, PAIRS + 1):
        pg[p] = jnp.zeros((2, C, 128), BF)
    edge[...] = jnp.zeros_like(edge)
    load_x.wait()
    for t in range(2 * PAIRS):
        pg[t // 2 + 1, t % 2] = move_tile(source, t, lambda i: x_ref[:, 128 * i:128 * i + 128], C)
    edge_columns(pg, edge, range(1, ROWS + 1))

    pl.semaphore_wait(barrier, greetings)

    def landed(ref, sem):
        pltpu.make_async_copy(ref, ref, sem).wait()

    def halo_copies(grid, edges, into, send, recv):
        copies = []
        for dl in (-1, 1, 0):
            for which, dn in ((0, -1), (1, 1)):
                copies.append(pltpu.make_async_remote_copy(
                    edges.at[which], into.at[3 + 3 * which + dl + 1], send, recv,
                    device_id={"lat": wrap(lat - dl, n_lat), "lon": wrap(lon + dn, n_lon)},
                    device_id_type=MESH))
        copies += [
            pltpu.make_async_remote_copy(
                grid.at[1], into.at[1:3], send, recv,
                device_id={"lat": wrap(lat - 1, n_lat)}, device_id_type=MESH),
            pltpu.make_async_remote_copy(
                grid.at[PAIRS, 0], into.at[0], send, recv,
                device_id={"lat": wrap(lat + 1, n_lat)}, device_id_type=MESH)]
        return copies

    halo = halo_copies(pg, edge, arrived, hs, hr)
    for copy in halo:
        copy.start()

    for copy in loads:
        copy.wait()
    wf[:, 9 * C:STACK] = jnp.zeros((F, STACK - 9 * C), BF)
    wb[...] = jnp.zeros_like(wb)
    strips = C * F // 128
    for i in range(strips):
        wrows[16 * i:16 * i + 9, :] = w_ref[:, 128 * i:128 * i + 128].astype(F32)
    channel = lax.broadcasted_iota(jnp.int32, (C, strips), 0)
    strip = lax.broadcasted_iota(jnp.int32, (C, strips), 1)
    begin = lax.shift_right_logical(channel * F, 7)
    pick = jnp.concatenate(
        [jnp.where(strip == begin + n, 1.0, 0.0).astype(BF) for n in range(2)], axis=0)
    strip_rows = jnp.concatenate(
        [wrows[pl.ds(i, strips, stride=16), :].astype(BF) for i in range(9)], axis=1)
    picked[...] = jnp.dot(pick, strip_rows, preferred_element_type=F32)
    offset = (lax.broadcasted_iota(jnp.int32, (C, 128), 0) * F) & 127
    from_first = lax.broadcasted_iota(jnp.int32, (C, 128), 1) >= offset
    for i in range(9):
        tap = jnp.where(from_first, picked[0:C, 128 * i:128 * i + 128],
                        picked[C:2 * C, 128 * i:128 * i + 128])
        for bit in (4, 8, 16, 32, 64):
            tap = jnp.where((offset & bit) != 0, pltpu.roll(tap, 128 - bit, 1), tap)
        tap = tap[:, :F]
        wb[:, C * i:C * i + F] = tap.astype(BF)
        wf[:, C * i:C * i + C] = tap.T.astype(BF)

    def as_column(row):
        square = lax.broadcasted_iota(jnp.int32, (F, F), 0) == lax.broadcasted_iota(jnp.int32, (F, F), 1)
        return jnp.sum(jnp.where(square, jnp.broadcast_to(row, (F, F)), 0.0), axis=1, keepdims=True)

    bias = as_column(bias_ref[...])
    fw = as_column(fw_ref[...])[None]

    acc[...] = jnp.zeros_like(acc)
    gedge[...] = jnp.zeros_like(gedge)
    load_an.wait()
    for t in range(2 * PAIRS):
        an_t[t // 2, t % 2] = move_tile(source, t, lambda i: an_ref[:, 128 * i:128 * i + 128], F)
    ones = jnp.ones((STACK - 9 * C, 256), BF)
    for p in range(PAIRS):
        stack[p, 9 * C:STACK, :] = ones

    landed(arrived, hr)
    landed(arrived, hs)
    place_halo(pg, arrived, lat, n_lat, range(10))

    def out_copy(k, j):
        dest = wrap(mem + j, n_mem)
        return pltpu.make_async_remote_copy(
            pred.at[k * 4 + dest], mv.at[k, j - 1], fs.at[k, j - 1], fr.at[k, j - 1],
            device_id={"member": dest}, device_id_type=MESH)

    def back_copy(k, j):
        dest = wrap(mem - j, n_mem)
        return pltpu.make_async_remote_copy(
            sc.at[k, j - 1], gg.at[k * 4 + mem + 1, :, 0:F, :], bs.at[k, j - 1], br.at[k, j - 1],
            device_id={"member": dest}, device_id_type=MESH)

    def back_arrival(k, j):
        return pltpu.make_async_remote_copy(
            sc.at[k, j - 1], gg.at[k * 4 + wrap(mem + j, n_mem) + 1, :, 0:F, :],
            bs.at[k, j - 1], br.at[k, j - 1],
            device_id={"member": wrap(mem - j, n_mem)}, device_id_type=MESH)

    def forward(k):
        def one(h, inner):
            p = k * 4 + 2 * h
            fill_stack(pg, p, 1, lambda n: stack.at[p + n])
            for n in range(2):
                out = jnp.dot(wf[...], stack[p + n], preferred_element_type=F32) + bias
                out = out.astype(BF)
                pred[p + n, 0] = out[:, :128]
                pred[p + n, 1] = out[:, 128:]
            return inner
        lax.fori_loop(0, 2, one, 0)
        for j in (2, 1, 3):
            out_copy(k, j).start()

    def score(k):
        own = k * 4 + mem
        for j in (1, 3, 2):
            out_copy(k, j).wait_recv()
        vals = [pred[own].astype(F32)] + [mv[k, j].astype(F32) for j in range(3)]
        target = an_t[own].astype(F32)
        pair = [None] * 4
        for i in range(4):
            for j in range(i + 1, 4):
                s = slope(vals[i] - vals[j])
                pair[i] = s if pair[i] is None else pair[i] + s
                pair[j] = -s if pair[j] is None else pair[j] - s
        for i in (2, 1, 3, 0):
            s = fw * (slope(vals[i] - target) * 0.25 - pair[i] / 12.0)
            if i == 0:
                gg[own + 1, :, 0:F, :] = s.astype(BF)
            else:
                sc[k, i - 1] = s.astype(BF)

    def send_back(k):
        for j in (2, 1, 3):
            back_copy(k, j).start()

    def weight_pair(p):
        g = jnp.concatenate([gg[p + 1, 0], gg[p + 1, 1]], axis=1)
        g = jnp.where(jnp.broadcast_to(interior(p), (C, 256)), g, jnp.zeros_like(g))
        acc[...] += lax.dot_general(g, stack[p], (((1,), (1,)), ((), ())), preferred_element_type=F32)

    ghalo = halo_copies(gg, gedge, garrived, gs, gr)

    def weights(k):
        weight_pair(k * 4 + mem)
        for j in (1, 3):
            back_arrival(k, j).wait_recv()
            weight_pair(k * 4 + wrap(mem + j, n_mem))
        back_arrival(k, 2).wait_recv()
        for chunk in range(CHUNKS):
            @pl.when(k == chunk)
            def _():
                edge_columns(gg, gedge, rows_of_chunk(chunk))
                if chunk == CHUNKS - 1:
                    for copy in ghalo:
                        copy.start()
        weight_pair(k * 4 + wrap(mem + 2, n_mem))

    def each(first, last, step):
        def run(k, carry):
            step(k)
            return carry
        lax.fori_loop(first, last, run, 0)

    each(0, 1, forward)
    place_halo(pg, arrived, lat, n_lat, range(10, 2 * PAIRS))
    each(1, CHUNKS, forward)
    each(0, EARLY, score)
    other_lat = lat + 1 - 2 * lax.rem(lat, 2)
    other_lon = z * 2 + 1 - y_lo
    for dev in ({"lat": other_lat}, {"lon": other_lon}, {"lat": other_lat, "lon": other_lon}):
        pl.semaphore_signal(pace, inc=1, device_id=dev, device_id_type=MESH)
    pl.semaphore_wait(pace, 3)
    each(0, EARLY, send_back)

    def late(k):
        score(k)
        send_back(k)

    each(EARLY, CHUNKS, late)
    each(0, CHUNKS, weights)

    for q in range(80):
        i, j = divmod(q, 7)
        ar0[q // 10, q % 10] = acc[8 * i:8 * i + 8, 128 * j:128 * j + 128] if q < 77 else jnp.zeros((8, 128), F32)

    def windows(t):
        return (t * 8) // 7

    def phase1(j):
        dest = wrap(lat + j, n_lat)
        return pltpu.make_async_remote_copy(
            ar0.at[dest], ar1.at[j - 1], s1, r1,
            device_id={"lat": dest}, device_id_type=MESH)

    def phase2(j):
        dest = wrap(z + j, n_z)
        return pltpu.make_async_remote_copy(
            a1.at[pl.ds(windows(dest), 2)], ar2.at[j - 1], s2, r2,
            device_id=at_z(dest), device_id_type=MESH)

    def phase3(j, slot):
        return pltpu.make_async_remote_copy(
            a2, ar3.at[slot], s3, r3,
            device_id=at_y(wrap(y + j, n_y)), device_id_type=MESH)

    def phase4(j, slot):
        return pltpu.make_async_remote_copy(
            ar4.at[z], ar4.at[slot], s4, r4,
            device_id=at_z(wrap(z + j, n_z)), device_id_type=MESH)

    def phase5(j, slot):
        return pltpu.make_async_remote_copy(
            ar5.at[lat], ar5.at[slot], s5, r5,
            device_id={"lat": wrap(lat + j, n_lat)}, device_id_type=MESH)

    far_first = (4, 3, 5, 2, 6, 1, 7)
    for j in far_first:
        phase1(j).start()

    def back(h, carry):
        p = 2 * h
        fill_stack(gg, p, -1, lambda n: bstack.at[n])
        for n in range(2):
            out = jnp.dot(wb[...], bstack[n], preferred_element_type=F32).astype(BF)
            gi_t[p + n, 0] = out[:, :128]
            gi_t[p + n, 1] = out[:, 128:]
        return carry

    landed(ar1, r1)
    total = ar0[lat]
    for j in range(n_lat - 1):
        total = total + ar1[j]
    a1[...] = total
    for j in far_first:
        phase2(j).start()

    landed(garrived, gr)
    landed(garrived, gs)
    place_halo(gg, garrived, lat, n_lat)

    lax.fori_loop(0, BACK[0], back, 0)
    landed(ar2, r2)
    total = a1[pl.ds(windows(z), 2)]
    for j in range(n_z - 1):
        total = total + ar2[j]
    a2[...] = total
    ar3[y] = total
    for j in far_first:
        phase3(j, y).start()

    lax.fori_loop(BACK[0], BACK[1], back, 0)
    landed(ar3.at[0:7], r3)
    total = ar3[0]
    for j in range(1, n_y):
        total = total + ar3[j]
    ar4[z] = total
    for j in far_first:
        phase4(j, z).start()

    lax.fori_loop(BACK[1], BACK[2], back, 0)
    landed(ar4.at[0:7], r4)
    for i in range(10):
        owner = max(t for t in range(8) if (t * 8) // 7 <= i)
        ar5[lat, i] = ar4[owner, i - (owner * 8) // 7]
    for j in far_first:
        phase5(j, lat).start()

    lax.fori_loop(BACK[2], PAIRS // 2, back, 0)
    dense = dense_source()
    for t in range(CELLS // 128):
        gi_ref[:, 128 * t:128 * t + 128] = move_tile(dense, t, lambda i: gi_t[i // 2, i % 2], C)
    store_gi = pltpu.make_async_copy(gi_ref, gi_hbm, io.at[2])
    store_gi.start()

    def sent(k):
        for j in (1, 2, 3):
            out_copy(k, j).wait_send()
            back_copy(k, j).wait_send()

    each(0, CHUNKS, sent)
    landed(ar1, s1)
    landed(ar2, s2)
    landed(ar2, s3)
    landed(ar2, s4)
    landed(ar5.at[0:7], r5)
    scale = 1.0 / (CELLS * n_lat * n_lon)
    for q in range(77):
        i, j = divmod(q, 7)
        full[8 * i:8 * i + 8, 128 * j:128 * j + 128] = ar5[q // 10, q % 10] * scale
    for j in range(7):
        turned = full[:, 128 * j:128 * j + 128].T
        if j < 6:
            gw_ref[128 * j:128 * j + 128, :] = turned[:, :F]
        else:
            gw_ref[128 * j:9 * C, :] = turned[:9 * C - 128 * j, :F]
            gb_ref[...] = turned[9 * C - 128 * j:9 * C - 128 * j + 1, :F]
    stores = [store_gi, pltpu.make_async_copy(gw_ref, gw_hbm, io.at[6]),
              pltpu.make_async_copy(gb_ref, gb_hbm, io.at[7])]
    for copy in stores[1:]:
        copy.start()
    landed(ar1, s5)
    for copy in stores:
        copy.wait()


def solution(mesh):
    sizes = tuple(mesh.shape[a] for a in ("member", "lat", "lon"))

    def local(inputs, weight, bias, analysis, field_weight):
        x = inputs[0, :, 0, 0]
        target = analysis[:, 0, 0]
        vm = pltpu.VMEM
        dma = pltpu.SemaphoreType.DMA
        halo = [vm((2, C, 128), BF), vm((9, C, 128), BF)]
        scratch = [
            vm((C, CELLS), BF),
            vm((F, CELLS), BF),
            vm((C, CELLS), BF),
            vm((9 * C, F), F32),
            vm((1, F), F32),
            vm((9, C * F), BF),
            vm((1, F), F32),
            vm((1, F), F32),
            vm((16 * (C * F // 128), 128), F32),
            vm((2 * C, 9 * 128), F32),
            vm((F, STACK), BF),
            vm((C, 9 * C), BF),
            vm((C, STACK), F32),
            vm((PAIRS + 2, 2, C, 128), BF),
            vm((PAIRS + 2, 2, C, 128), BF),
            vm((PAIRS, STACK, 256), BF),
            vm((2, 9 * C, 256), BF),
            vm((PAIRS, 2, F, 128), BF),
            vm((CHUNKS, 3, 2, F, 128), BF),
            vm((CHUNKS, 3, 2, F, 128), BF),
            vm((PAIRS, 2, F, 128), BF),
            vm((C, STACK), F32),
            vm((PAIRS, 2, C, 128), BF),
            *halo, *halo,
            vm((8, 10, 8, 128), F32),
            vm((7, 10, 8, 128), F32),
            vm((7, 2, 8, 128), F32),
            vm((10, 8, 128), F32),
            vm((2, 8, 128), F32),
            vm((8, 2, 8, 128), F32),
            vm((8, 2, 8, 128), F32),
            vm((8, 10, 8, 128), F32),
            pltpu.SemaphoreType.REGULAR,
            dma((8,)), dma, dma, dma, dma,
            *[dma((CHUNKS, 3))] * 4,
            *[dma] * 10,
        ]

        def body(*refs):
            kernel(sizes, *refs)

        stay = pl.BlockSpec(memory_space=pltpu.HBM)
        gi, gw, gb = pl.pallas_call(
            body,
            out_shape=(jax.ShapeDtypeStruct((C, CELLS), BF), jax.ShapeDtypeStruct((9 * C, F), F32),
                       jax.ShapeDtypeStruct((1, F), F32)),
            in_specs=[stay] * 5,
            out_specs=[pl.BlockSpec(memory_space=pl.ANY)] * 3,
            scratch_shapes=scratch,
            compiler_params=pltpu.CompilerParams(
                collective_id=0, has_side_effects=True, vmem_limit_bytes=32 * 2**20),
        )(*(pltpu.with_memory_space_constraint(v, pltpu.HBM) for v in (x, target, weight, bias[None], field_weight[None])))
        return gi.reshape(1, C, 1, 1, CELLS), gw.reshape(9, C * F), gb[0]

    placed = (P("member", None, "lat", "lon", None), P(), P(), P(None, "lat", "lon", None), P())
    return jax.shard_map(
        local,
        mesh=mesh,
        in_specs=placed,
        out_specs=(P("member", None, "lat", "lon", None), P(), P()),
        check_vma=False,
    )
```

```python
import numpy as np
import jax
import jax.numpy as jnp
from jax import lax
from jax.experimental import pallas as pl
from jax.experimental.pallas import tpu as pltpu
from jax.sharding import PartitionSpec as P

MESH = pl.DeviceIdType.MESH
C, F, ROWS, COLS = 96, 84, 64, 90
CELLS = ROWS * COLS
PITCH = COLS + 2
PAIRS = 24
CHUNKS = 6
STACK = 896
EARLY = 1
BACK = (3, 6, 9)
BF, F32 = jnp.bfloat16, jnp.float32
TAPS = [(a, b) for a in range(3) for b in range(3)]


def padded_source():
    lane = np.arange(PAIRS * 256)
    r, c = lane // PITCH, lane % PITCH
    inside = (r >= 1) & (r <= ROWS) & (c >= 1) & (c <= COLS)
    return np.where(inside, COLS * (r - 1) + c - 1, -1)


def dense_source():
    cell = np.arange(CELLS)
    return PITCH * (cell // COLS + 1) + cell % COLS + 1


def segments(source, tile):
    out = []
    for lane in range(128):
        src = source[tile * 128 + lane]
        key = (None, 0) if src < 0 else (int(src) // 128, int(lane - src) % 128)
        if not out or out[-1][1:] != key:
            out.append((lane,) + key)
    return out


def move_tile(source, tile, load, rows):
    lane = lax.broadcasted_iota(jnp.int32, (rows, 128), 1)
    acc = None
    for first, src, shift in segments(source, tile):
        if src is None:
            val = jnp.zeros((rows, 128), BF)
        else:
            val = load(src)
            if shift:
                val = pltpu.roll(val, shift, 1)
        acc = val if acc is None else jnp.where(lane >= first, val, acc)
    return acc


def lane_grid(p):
    o = p * 256 + lax.broadcasted_iota(jnp.int32, (1, 256), 1)
    r = lax.shift_right_logical(o * 45591, 22)
    c = o - r * PITCH
    return r, c


def interior(p):
    r, c = lane_grid(p)
    return (r >= 1) & (r <= ROWS) & (c >= 1) & (c <= COLS)


def slope(u):
    return u * lax.rsqrt(u * u + 1.0)


def edge_columns(grid, edges, rows):
    lane = lax.broadcasted_iota(jnp.int32, (C, 128), 1)
    found = [edges[0], edges[1]]
    for r in rows:
        for which, col in enumerate((1, COLS)):
            o = PITCH * r + col
            t, l = o // 128, o % 128
            val = grid[t // 2 + 1, t % 2]
            val = pltpu.roll(val, (r - l) % 128, 1)
            found[which] = jnp.where(lane == r, val, found[which])
    edges[0] = found[0]
    edges[1] = found[1]


def rows_of_chunk(k):
    return [r for r in range(1, ROWS + 1) if (PITCH * r + COLS) // (256 * 4) == k]


def place_halo(grid, arrived, lat, n_lat, tiles=range(2 * PAIRS)):
    lane = lax.broadcasted_iota(jnp.int32, (C, 128), 1)
    zero = jnp.zeros((C, 128), BF)
    has_top = jnp.where(lat > 0, 1, 0)
    has_bottom = jnp.where(lat < n_lat - 1, 1, 0)
    top_on = jnp.broadcast_to(has_top, (C, 128)) == 1
    bottom_on = jnp.broadcast_to(has_bottom, (C, 128)) == 1

    def column(at):
        above, own, below = (arrived[at + i] for i in range(3))
        val = jnp.where((lane >= 1) & (lane <= ROWS), own, zero)
        val = jnp.where((lane == 0) & top_on, pltpu.roll(above, 64, 1), val)
        return jnp.where((lane == ROWS + 1) & bottom_on, pltpu.roll(below, 64, 1), val)

    cl, cr = column(6), column(3)
    for t in tiles:
        base = grid[t // 2 + 1, t % 2]
        if t == 0:
            base = jnp.where((lane >= 1) & (lane <= COLS), jnp.where(top_on, arrived[0], zero), base)
        if t == 46:
            base = jnp.where(lane >= 93, jnp.where(bottom_on, arrived[1], zero), base)
        if t == 47:
            base = jnp.where(lane <= 54, jnp.where(bottom_on, arrived[2], zero), base)
        for l in range(128):
            r, c = divmod(t * 128 + l, PITCH)
            if r > ROWS + 1:
                continue
            if c == 0:
                base = jnp.where(lane == l, pltpu.roll(cl, (l - r) % 128, 1), base)
            if c == PITCH - 1:
                base = jnp.where(lane == l, pltpu.roll(cr, (l - r) % 128, 1), base)
        grid[t // 2 + 1, t % 2] = base


def fill_stack(grid, p, sign, dst):
    lane = lax.broadcasted_iota(jnp.int32, (C, 128), 1)
    tiles = (grid[p, 1], grid[p + 1, 0], grid[p + 1, 1], grid[p + 2, 0], grid[p + 2, 1], grid[p + 3, 0])
    for i, (a, b) in enumerate(TAPS):
        d = sign * (PITCH * (a - 1) + b - 1)
        if d == 0:
            win = tiles[1:5]
        else:
            base, s = (0, d + 128) if d < 0 else (1, d)
            rolled = [pltpu.roll(tiles[base + n], 128 - s, 1) for n in range(5)]
            keep = lane < 128 - s
            win = [jnp.where(keep, rolled[n], rolled[n + 1]) for n in range(4)]
        for n in range(4):
            dst(n // 2)[C * i:C * i + C, 128 * (n % 2):128 * (n % 2) + 128] = win[n]


def kernel(sizes, x_hbm, an_hbm, w_hbm, bias_hbm, fw_hbm, gi_hbm, gw_hbm, gb_hbm,
           x_ref, an_ref, gi_ref, gw_ref, gb_ref, w_ref, bias_ref, fw_ref, wrows, picked, wf, wb, full,
           pg, gg, stack, bstack, pred, mv, sc, an_t, acc, gi_t,
           edge, arrived, gedge, garrived,
           ar0, ar1, ar2, a1, a2, ar3, ar4, ar5,
           pace, io, hs, hr, gs, gr, fs, fr, bs, br,
           s1, r1, s2, r2, s3, r3, s4, r4, s5, r5):
    n_mem, n_lat, n_lon = sizes
    n_z, n_y = n_lon // 2, n_mem * 2
    mem, lat, lon = (lax.axis_index(a) for a in ("member", "lat", "lon"))
    z, y_lo = lon // 2, lax.rem(lon, 2)
    y = mem * 2 + y_lo

    third = CELLS // 3
    load_x = [pltpu.make_async_copy(
        x_hbm.at[:, third * i:third * i + third], x_ref.at[:, third * i:third * i + third],
        io.at[(0, 8, 9)[i]]) for i in range(3)]
    load_an = pltpu.make_async_copy(an_hbm, an_ref, io.at[1])
    loads = [pltpu.make_async_copy(src, dst, io.at[3 + i]) for i, (src, dst) in enumerate(
        ((w_hbm, w_ref), (bias_hbm, bias_ref), (fw_hbm, fw_ref)))]
    for copy in load_x:
        copy.start()
    for copy in loads:
        copy.start()
    load_an.start()

    def wrap(v, n):
        return lax.rem(v + n, n)

    def at_y(t):
        return {"member": t // 2, "lon": z * 2 + lax.rem(t, 2)}

    def at_z(t):
        return {"lon": t * 2 + y_lo}

    zeros12 = jnp.zeros((2, C - F, 128), BF)
    for p in range(PAIRS + 2):
        gg[p, :, F:C, :] = zeros12
    for p in (0, PAIRS + 1):
        gg[p, :, 0:F, :] = jnp.zeros((2, F, 128), BF)

    barrier = pltpu.get_barrier_semaphore()

    def greet(dev):
        pl.semaphore_signal(barrier, inc=1, device_id=dev, device_id_type=MESH)

    for dl in (-1, 0, 1):
        for dn in (-1, 1):
            greet({"lat": wrap(lat + dl, n_lat), "lon": wrap(lon + dn, n_lon)})
    for j in range(1, n_lat):
        greet({"lat": wrap(lat + j, n_lat)})
    for j in range(1, n_z):
        greet(at_z(wrap(z + j, n_z)))
    for j in range(1, n_y):
        greet(at_y(wrap(y + j, n_y)))
    greetings = n_lat - 1 + n_z - 1 + n_y - 1 + 6

    source = padded_source()
    for p in (0, PAIRS + 1):
        pg[p] = jnp.zeros((2, C, 128), BF)
    edge[...] = jnp.zeros_like(edge)
    load_x[0].wait()
    here = 0
    for t in range(2 * PAIRS):
        while here < 2 and source[128 * t:128 * t + 128].max() >= third * (here + 1):
            here += 1
            load_x[here].wait()
        pg[t // 2 + 1, t % 2] = move_tile(source, t, lambda i: x_ref[:, 128 * i:128 * i + 128], C)
    edge_columns(pg, edge, range(1, ROWS + 1))

    pl.semaphore_wait(barrier, greetings)

    def landed(ref, sem):
        pltpu.make_async_copy(ref, ref, sem).wait()

    def halo_copies(grid, edges, into, send, recv):
        copies = []
        for dl in (-1, 1, 0):
            for which, dn in ((0, -1), (1, 1)):
                copies.append(pltpu.make_async_remote_copy(
                    edges.at[which], into.at[3 + 3 * which + dl + 1], send, recv,
                    device_id={"lat": wrap(lat - dl, n_lat), "lon": wrap(lon + dn, n_lon)},
                    device_id_type=MESH))
        copies += [
            pltpu.make_async_remote_copy(
                grid.at[1], into.at[1:3], send, recv,
                device_id={"lat": wrap(lat - 1, n_lat)}, device_id_type=MESH),
            pltpu.make_async_remote_copy(
                grid.at[PAIRS, 0], into.at[0], send, recv,
                device_id={"lat": wrap(lat + 1, n_lat)}, device_id_type=MESH)]
        return copies

    halo = halo_copies(pg, edge, arrived, hs, hr)
    for copy in halo:
        copy.start()

    for copy in loads:
        copy.wait()
    wf[:, 9 * C:STACK] = jnp.zeros((F, STACK - 9 * C), BF)
    wb[...] = jnp.zeros_like(wb)
    strips = C * F // 128
    for i in range(strips):
        wrows[16 * i:16 * i + 9, :] = w_ref[:, 128 * i:128 * i + 128].astype(F32)
    channel = lax.broadcasted_iota(jnp.int32, (C, strips), 0)
    strip = lax.broadcasted_iota(jnp.int32, (C, strips), 1)
    begin = lax.shift_right_logical(channel * F, 7)
    pick = jnp.concatenate(
        [jnp.where(strip == begin + n, 1.0, 0.0).astype(BF) for n in range(2)], axis=0)
    strip_rows = jnp.concatenate(
        [wrows[pl.ds(i, strips, stride=16), :].astype(BF) for i in range(9)], axis=1)
    picked[...] = jnp.dot(pick, strip_rows, preferred_element_type=F32)
    offset = (lax.broadcasted_iota(jnp.int32, (C, 128), 0) * F) & 127
    from_first = lax.broadcasted_iota(jnp.int32, (C, 128), 1) >= offset
    for i in range(9):
        tap = jnp.where(from_first, picked[0:C, 128 * i:128 * i + 128],
                        picked[C:2 * C, 128 * i:128 * i + 128])
        for bit in (4, 8, 16, 32, 64):
            tap = jnp.where((offset & bit) != 0, pltpu.roll(tap, 128 - bit, 1), tap)
        tap = tap[:, :F]
        wb[:, C * i:C * i + F] = tap.astype(BF)
        wf[:, C * i:C * i + C] = tap.T.astype(BF)

    def as_column(row):
        square = lax.broadcasted_iota(jnp.int32, (F, F), 0) == lax.broadcasted_iota(jnp.int32, (F, F), 1)
        return jnp.sum(jnp.where(square, jnp.broadcast_to(row, (F, F)), 0.0), axis=1, keepdims=True)

    bias = as_column(bias_ref[...])
    fw = as_column(fw_ref[...])[None]

    acc[...] = jnp.zeros_like(acc)
    gedge[...] = jnp.zeros_like(gedge)
    load_an.wait()
    for t in range(2 * PAIRS):
        an_t[t // 2, t % 2] = move_tile(source, t, lambda i: an_ref[:, 128 * i:128 * i + 128], F)
    ones = jnp.ones((STACK - 9 * C, 256), BF)
    for p in range(PAIRS):
        stack[p, 9 * C:STACK, :] = ones

    landed(arrived, hr)
    landed(arrived, hs)
    place_halo(pg, arrived, lat, n_lat, range(10))

    def out_copy(k, j):
        dest = wrap(mem + j, n_mem)
        return pltpu.make_async_remote_copy(
            pred.at[k * 4 + dest], mv.at[k, j - 1], fs.at[k, j - 1], fr.at[k, j - 1],
            device_id={"member": dest}, device_id_type=MESH)

    def back_copy(k, j):
        dest = wrap(mem - j, n_mem)
        return pltpu.make_async_remote_copy(
            sc.at[k, j - 1], gg.at[k * 4 + mem + 1, :, 0:F, :], bs.at[k, j - 1], br.at[k, j - 1],
            device_id={"member": dest}, device_id_type=MESH)

    def back_arrival(k, j):
        return pltpu.make_async_remote_copy(
            sc.at[k, j - 1], gg.at[k * 4 + wrap(mem + j, n_mem) + 1, :, 0:F, :],
            bs.at[k, j - 1], br.at[k, j - 1],
            device_id={"member": wrap(mem - j, n_mem)}, device_id_type=MESH)

    def forward(k):
        def one(h, inner):
            p = k * 4 + 2 * h
            fill_stack(pg, p, 1, lambda n: stack.at[p + n])
            for n in range(2):
                out = jnp.dot(wf[...], stack[p + n], preferred_element_type=F32) + bias
                out = out.astype(BF)
                pred[p + n, 0] = out[:, :128]
                pred[p + n, 1] = out[:, 128:]
            return inner
        lax.fori_loop(0, 2, one, 0)
        for j in (2, 1, 3):
            out_copy(k, j).start()

    def score(k):
        own = k * 4 + mem
        for j in (1, 3, 2):
            out_copy(k, j).wait_recv()
        vals = [pred[own].astype(F32)] + [mv[k, j].astype(F32) for j in range(3)]
        target = an_t[own].astype(F32)
        pair = [None] * 4
        for i in range(4):
            for j in range(i + 1, 4):
                s = slope(vals[i] - vals[j])
                pair[i] = s if pair[i] is None else pair[i] + s
                pair[j] = -s if pair[j] is None else pair[j] - s
        for i in (2, 1, 3, 0):
            s = fw * (slope(vals[i] - target) * 0.25 - pair[i] / 12.0)
            if i == 0:
                gg[own + 1, :, 0:F, :] = s.astype(BF)
            else:
                sc[k, i - 1] = s.astype(BF)

    def send_back(k):
        for j in (2, 1, 3):
            back_copy(k, j).start()

    def weight_pair(p):
        g = jnp.concatenate([gg[p + 1, 0], gg[p + 1, 1]], axis=1)
        g = jnp.where(jnp.broadcast_to(interior(p), (C, 256)), g, jnp.zeros_like(g))
        acc[...] += lax.dot_general(g, stack[p], (((1,), (1,)), ((), ())), preferred_element_type=F32)

    ghalo = halo_copies(gg, gedge, garrived, gs, gr)

    def weights(k):
        weight_pair(k * 4 + mem)
        for j in (1, 3):
            back_arrival(k, j).wait_recv()
            weight_pair(k * 4 + wrap(mem + j, n_mem))
        back_arrival(k, 2).wait_recv()
        for chunk in range(CHUNKS):
            @pl.when(k == chunk)
            def _():
                edge_columns(gg, gedge, rows_of_chunk(chunk))
                if chunk == CHUNKS - 1:
                    for copy in ghalo:
                        copy.start()
        weight_pair(k * 4 + wrap(mem + 2, n_mem))

    def each(first, last, step):
        def run(k, carry):
            step(k)
            return carry
        lax.fori_loop(first, last, run, 0)

    each(0, 1, forward)
    place_halo(pg, arrived, lat, n_lat, range(10, 2 * PAIRS))
    each(1, CHUNKS, forward)
    each(0, EARLY, score)
    other_lat = lat + 1 - 2 * lax.rem(lat, 2)
    other_lon = z * 2 + 1 - y_lo
    for dev in ({"lat": other_lat}, {"lon": other_lon}, {"lat": other_lat, "lon": other_lon}):
        pl.semaphore_signal(pace, inc=1, device_id=dev, device_id_type=MESH)
    pl.semaphore_wait(pace, 3)
    each(0, EARLY, send_back)

    def late(k):
        score(k)
        send_back(k)

    each(EARLY, CHUNKS, late)
    each(0, CHUNKS, weights)

    for q in range(80):
        i, j = divmod(q, 7)
        ar0[q // 10, q % 10] = acc[8 * i:8 * i + 8, 128 * j:128 * j + 128] if q < 77 else jnp.zeros((8, 128), F32)

    def windows(t):
        return (t * 8) // 7

    def phase1(j):
        dest = wrap(lat + j, n_lat)
        return pltpu.make_async_remote_copy(
            ar0.at[dest], ar1.at[j - 1], s1, r1,
            device_id={"lat": dest}, device_id_type=MESH)

    def phase2(j):
        dest = wrap(z + j, n_z)
        return pltpu.make_async_remote_copy(
            a1.at[pl.ds(windows(dest), 2)], ar2.at[j - 1], s2, r2,
            device_id=at_z(dest), device_id_type=MESH)

    def phase3(j, slot):
        return pltpu.make_async_remote_copy(
            a2, ar3.at[slot], s3, r3,
            device_id=at_y(wrap(y + j, n_y)), device_id_type=MESH)

    def phase4(j, slot):
        return pltpu.make_async_remote_copy(
            ar4.at[z], ar4.at[slot], s4, r4,
            device_id=at_z(wrap(z + j, n_z)), device_id_type=MESH)

    def phase5(j, slot):
        return pltpu.make_async_remote_copy(
            ar5.at[lat], ar5.at[slot], s5, r5,
            device_id={"lat": wrap(lat + j, n_lat)}, device_id_type=MESH)

    far_first = (4, 3, 5, 2, 6, 1, 7)
    for j in far_first:
        phase1(j).start()

    def back(h, carry):
        p = 2 * h
        fill_stack(gg, p, -1, lambda n: bstack.at[n])
        for n in range(2):
            out = jnp.dot(wb[...], bstack[n], preferred_element_type=F32).astype(BF)
            gi_t[p + n, 0] = out[:, :128]
            gi_t[p + n, 1] = out[:, 128:]
        return carry

    landed(ar1, r1)
    total = ar0[lat]
    for j in range(n_lat - 1):
        total = total + ar1[j]
    a1[...] = total
    for j in far_first:
        phase2(j).start()

    landed(garrived, gr)
    landed(garrived, gs)
    place_halo(gg, garrived, lat, n_lat)

    lax.fori_loop(0, BACK[0], back, 0)
    landed(ar2, r2)
    total = a1[pl.ds(windows(z), 2)]
    for j in range(n_z - 1):
        total = total + ar2[j]
    a2[...] = total
    ar3[y] = total
    for j in far_first:
        phase3(j, y).start()

    lax.fori_loop(BACK[0], BACK[1], back, 0)
    landed(ar3.at[0:7], r3)
    total = ar3[0]
    for j in range(1, n_y):
        total = total + ar3[j]
    ar4[z] = total
    for j in far_first:
        phase4(j, z).start()

    lax.fori_loop(BACK[1], BACK[2], back, 0)
    landed(ar4.at[0:7], r4)
    for i in range(10):
        owner = max(t for t in range(8) if (t * 8) // 7 <= i)
        ar5[lat, i] = ar4[owner, i - (owner * 8) // 7]
    for j in far_first:
        phase5(j, lat).start()

    lax.fori_loop(BACK[2], PAIRS // 2, back, 0)
    dense = dense_source()
    for t in range(CELLS // 128):
        gi_ref[:, 128 * t:128 * t + 128] = move_tile(dense, t, lambda i: gi_t[i // 2, i % 2], C)
    store_gi = pltpu.make_async_copy(gi_ref, gi_hbm, io.at[2])
    store_gi.start()

    def sent(k):
        for j in (1, 2, 3):
            out_copy(k, j).wait_send()
            back_copy(k, j).wait_send()

    each(0, CHUNKS, sent)
    landed(ar1, s1)
    landed(ar2, s2)
    landed(ar2, s3)
    landed(ar2, s4)
    landed(ar5.at[0:7], r5)
    scale = 1.0 / (CELLS * n_lat * n_lon)
    for q in range(77):
        i, j = divmod(q, 7)
        full[8 * i:8 * i + 8, 128 * j:128 * j + 128] = ar5[q // 10, q % 10] * scale
    for j in range(7):
        turned = full[:, 128 * j:128 * j + 128].T
        if j < 6:
            gw_ref[128 * j:128 * j + 128, :] = turned[:, :F]
        else:
            gw_ref[128 * j:9 * C, :] = turned[:9 * C - 128 * j, :F]
            gb_ref[...] = turned[9 * C - 128 * j:9 * C - 128 * j + 1, :F]
    stores = [store_gi, pltpu.make_async_copy(gw_ref, gw_hbm, io.at[6]),
              pltpu.make_async_copy(gb_ref, gb_hbm, io.at[7])]
    for copy in stores[1:]:
        copy.start()
    landed(ar1, s5)
    for copy in stores:
        copy.wait()


def solution(mesh):
    sizes = tuple(mesh.shape[a] for a in ("member", "lat", "lon"))

    def local(inputs, weight, bias, analysis, field_weight):
        x = inputs[0, :, 0, 0]
        target = analysis[:, 0, 0]
        vm = pltpu.VMEM
        dma = pltpu.SemaphoreType.DMA
        halo = [vm((2, C, 128), BF), vm((9, C, 128), BF)]
        scratch = [
            vm((C, CELLS), BF),
            vm((F, CELLS), BF),
            vm((C, CELLS), BF),
            vm((9 * C, F), F32),
            vm((1, F), F32),
            vm((9, C * F), BF),
            vm((1, F), F32),
            vm((1, F), F32),
            vm((16 * (C * F // 128), 128), F32),
            vm((2 * C, 9 * 128), F32),
            vm((F, STACK), BF),
            vm((C, 9 * C), BF),
            vm((C, STACK), F32),
            vm((PAIRS + 2, 2, C, 128), BF),
            vm((PAIRS + 2, 2, C, 128), BF),
            vm((PAIRS, STACK, 256), BF),
            vm((2, 9 * C, 256), BF),
            vm((PAIRS, 2, F, 128), BF),
            vm((CHUNKS, 3, 2, F, 128), BF),
            vm((CHUNKS, 3, 2, F, 128), BF),
            vm((PAIRS, 2, F, 128), BF),
            vm((C, STACK), F32),
            vm((PAIRS, 2, C, 128), BF),
            *halo, *halo,
            vm((8, 10, 8, 128), F32),
            vm((7, 10, 8, 128), F32),
            vm((7, 2, 8, 128), F32),
            vm((10, 8, 128), F32),
            vm((2, 8, 128), F32),
            vm((8, 2, 8, 128), F32),
            vm((8, 2, 8, 128), F32),
            vm((8, 10, 8, 128), F32),
            pltpu.SemaphoreType.REGULAR,
            dma((10,)), dma, dma, dma, dma,
            *[dma((CHUNKS, 3))] * 4,
            *[dma] * 10,
        ]

        def body(*refs):
            kernel(sizes, *refs)

        stay = pl.BlockSpec(memory_space=pltpu.HBM)
        gi, gw, gb = pl.pallas_call(
            body,
            out_shape=(jax.ShapeDtypeStruct((C, CELLS), BF), jax.ShapeDtypeStruct((9 * C, F), F32),
                       jax.ShapeDtypeStruct((1, F), F32)),
            in_specs=[stay] * 5,
            out_specs=[pl.BlockSpec(memory_space=pl.ANY)] * 3,
            scratch_shapes=scratch,
            compiler_params=pltpu.CompilerParams(
                collective_id=0, has_side_effects=True, vmem_limit_bytes=32 * 2**20),
        )(*(pltpu.with_memory_space_constraint(v, pltpu.HBM) for v in (x, target, weight, bias[None], field_weight[None])))
        return gi.reshape(1, C, 1, 1, CELLS), gw.reshape(9, C * F), gb[0]

    placed = (P("member", None, "lat", "lon", None), P(), P(), P(None, "lat", "lon", None), P())
    return jax.shard_map(
        local,
        mesh=mesh,
        in_specs=placed,
        out_specs=(P("member", None, "lat", "lon", None), P(), P()),
        check_vma=False,
    )
```
